32 devices in a mesh: rep: 4 (over z), fsdp: 4 (over y, core), seq: 2 (over x).
Axes of the slice: x: 2, y: 2, z: 4, core: 2. Of those that a mesh axis runs over, the one named last changes fastest.
Arguments:
- images: bfloat16 [16, 576, 768], P(('rep', 'fsdp'), 'seq'), may hold values from -6 to 6
- cotangent: bfloat16 [16, 576, 768], P(('rep', 'fsdp'), 'seq'), may hold values from -6 to 6
- first_gain: bfloat16 [768], P(('fsdp', 'seq')), may hold values from 0.25 to 1.75
- first_shift: bfloat16 [768], P(('fsdp', 'seq')), may hold values from -3 to 3
- input_weight: bfloat16 [768, 2304], P(('fsdp', 'seq')), may hold values from -0.21875 to 0.21875
- query_bias: bfloat16 [768], P(('fsdp', 'seq')), may hold values from -3 to 3
- value_bias: bfloat16 [768], P(('fsdp', 'seq')), may hold values from -0.29882812 to 0.29882812
- output_weight: bfloat16 [768, 768], P(('fsdp', 'seq')), may hold values from -2.5 to 2.5
- output_bias: bfloat16 [768], P(('fsdp', 'seq')), may hold values from -3 to 3
- second_gain: bfloat16 [768], P(('fsdp', 'seq')), may hold values from 0.25 to 1.75
- second_shift: bfloat16 [768], P(('fsdp', 'seq')), may hold values from -3 to 3
- up_weight: bfloat16 [768, 3072], P(('fsdp', 'seq')), may hold values from -0.21875 to 0.21875
- up_bias: bfloat16 [3072], P(('fsdp', 'seq')), may hold values from -3 to 3
- down_weight: bfloat16 [3072, 768], P(('fsdp', 'seq')), may hold values from -0.109375 to 0.109375
- down_bias: bfloat16 [768], P(('fsdp', 'seq')), may hold values from -3 to 3
Outputs:
- layer_out: bfloat16 [16, 576, 768], P(('rep', 'fsdp'), 'seq')
- input_gradient: float32 [16, 576, 768], P(('rep', 'fsdp'), 'seq')
- first_gain_gradient: float32 [768], P(('fsdp', 'seq'))
- first_shift_gradient: float32 [768], P(('fsdp', 'seq'))
- input_weight_gradient: float32 [768, 2304], P(('fsdp', 'seq'))
- query_bias_gradient: float32 [768], P(('fsdp', 'seq'))
- value_bias_gradient: float32 [768], P(('fsdp', 'seq'))
- output_weight_gradient: float32 [768, 768], P(('fsdp', 'seq'))
- output_bias_gradient: float32 [768], P(('fsdp', 'seq'))
- second_gain_gradient: float32 [768], P(('fsdp', 'seq'))
- second_shift_gradient: float32 [768], P(('fsdp', 'seq'))
- up_weight_gradient: float32 [768, 3072], P(('fsdp', 'seq'))
- up_bias_gradient: float32 [3072], P(('fsdp', 'seq'))
- down_weight_gradient: float32 [3072, 768], P(('fsdp', 'seq'))
- down_bias_gradient: float32 [768], P(('fsdp', 'seq'))
The draws below stay inside these ranges and needn't reach their ends.
All inputs are finite; a program needn't handle non-finite values.
Results may differ from the reference program's by a relative error of at most 0.011.
Values may be sent and summed in bfloat16 or wider, within the bound.
A program may use at most 128 MiB of HBM per device.

```python
import math
import jax
import jax.numpy as jnp
from jax import lax

D = 768
FF = 3072
HEADS = 12
SEQ_LEN = 576
IMAGES = 16


def with_spikes(drawn, stream_key, source, target, shards_of, factor):
    def block_of(dim):
        return (jnp.arange(drawn.shape[dim]) // (drawn.shape[dim] // shards_of)).reshape((-1,) + (1,) * (drawn.ndim - 1 - dim))

    near = jax.random.permutation(stream_key, shards_of)[block_of(target)]
    second = (block_of(target) + shards_of // 2) % shards_of
    return jnp.where((block_of(source) == near) | (block_of(source) == second), factor * drawn, drawn)


def steps_of(key, extent, shards, least, top_value):
    def one(dim, blocks):
        draws = jax.random.uniform(jax.random.fold_in(jax.random.fold_in(key, 6), dim), (blocks,), jnp.float32, least / len(shards), top_value / len(shards))
        return jnp.repeat(jnp.exp(draws), extent[dim] // blocks).reshape((-1,) + (1,) * (len(extent) - dim - 1))

    factor_of = one(*shards[0])
    for cut in shards[1:]:
        factor_of = factor_of * one(*cut)
    return factor_of


def bell_draw(rng, shape, width, reach, pieces=(), held_as=jnp.bfloat16):
    result = width * jax.random.normal(rng, shape, jnp.float32)
    if pieces:
        result = result * steps_of(rng, shape, pieces, -0.22, 0.18)
    return jnp.clip(result, -reach, reach).astype(held_as)


def gaussian_with(key, shape, scale, most, shards, heavy, held_as=jnp.bfloat16):
    values = scale * jax.random.normal(key, shape, jnp.float32)
    if shards:
        values = values * steps_of(key, shape, shards, -0.22, 0.18)
    return jnp.clip(with_spikes(values, jax.random.fold_in(key, 3), *heavy), -most, most).astype(held_as)


def setup_inputs(seed: int = 0) -> dict:
    key_of = jax.random.split(jax.random.key(seed), 16)
    images = gaussian_with(key_of[0], (IMAGES, SEQ_LEN, D), 1.0, 6.0, ((0, 16), (1, 2)), (0, 2, 16, 2.0))
    cotangent = gaussian_with(key_of[1], (IMAGES, SEQ_LEN, D), 1.0, 6.0, ((0, 16), (1, 2)), (0, 2, 16, 2.0))
    first_gain = jnp.clip(1.0 + 0.15 * jax.random.normal(key_of[2], (D,), jnp.float32), 0.25, 1.75).astype(jnp.bfloat16)
    first_shift = bell_draw(key_of[3], (D,), 0.3, 3.0, ((0, 8),))
    input_weight = bell_draw(key_of[4], (D, 3 * D), D ** -0.5, 0.21875, ((0, 8),))
    query_bias = bell_draw(key_of[5], (D,), 0.5, 3.0, ((0, 8),))
    value_bias = bell_draw(key_of[6], (D,), 0.05, 0.29882812, ((0, 8),))
    output_weight = bell_draw(key_of[7], (D, D), (max(1, 4 * D // SEQ_LEN)) ** -0.5, 2.5, ((0, 8),))
    output_bias = bell_draw(key_of[8], (D,), 0.5, 3.0, ((0, 8),))
    second_gain = jnp.clip(1.0 + 0.15 * jax.random.normal(key_of[9], (D,), jnp.float32), 0.25, 1.75).astype(jnp.bfloat16)
    second_shift = bell_draw(key_of[10], (D,), 0.3, 3.0, ((0, 8),))
    up_weight = bell_draw(key_of[11], (D, FF), D ** -0.5, 0.21875, ((0, 8),))
    up_bias = bell_draw(key_of[12], (FF,), 0.5, 3.0, ((0, 8),))
    down_weight = bell_draw(key_of[13], (FF, D), FF ** -0.5, 0.109375, ((0, 8),))
    down_bias = bell_draw(key_of[14], (D,), 0.5, 3.0, ((0, 8),))
    return {"images": images, "cotangent": cotangent, "first_gain": first_gain, "first_shift": first_shift, "input_weight": input_weight, "query_bias": query_bias, "value_bias": value_bias, "output_weight": output_weight, "output_bias": output_bias, "second_gain": second_gain, "second_shift": second_shift, "up_weight": up_weight, "up_bias": up_bias, "down_weight": down_weight, "down_bias": down_bias}


@jax.custom_vjp
def low(v):
    return lax.optimization_barrier(v.astype(jnp.bfloat16)).astype(jnp.float32)

@jax.custom_vjp
def low_back(v):
    return v

def low_keep(v):
    return (low(v), None)

def low_pass(kept, grad):
    return (grad,)

def back_keep(v):
    return (v, None)

def back_low(kept, grad):
    return (low(grad),)
low.defvjp(low_keep, low_pass)
low_back.defvjp(back_keep, back_low)
EPSILON = 1e-06

def both_ways(tensor):
    return low(low_back(tensor))

def normalize(features, scale_gain, shift_bias):
    row_mean = lax.optimization_barrier(jnp.mean(features, axis=-1, keepdims=True))
    centred = features - row_mean
    row_var = lax.optimization_barrier(jnp.mean(centred * centred, axis=-1, keepdims=True))
    return centred * lax.rsqrt(row_var + EPSILON) * scale_gain + shift_bias

def matmul(first_operand, second_operand):
    return jnp.einsum('gtk,kn->gtn', first_operand, second_operand, precision=lax.Precision.HIGHEST)

def forward(images, params):
    first_gain, first_shift, input_weight, query_bias, value_bias, output_weight, output_bias, second_gain, second_shift, up_weight, up_bias, down_weight, down_bias = params
    groups, length, feature_width = images.shape
    head_size = feature_width // HEADS
    score_scale = 1.0 / math.sqrt(head_size)
    normed = low(normalize(images, first_gain, first_shift))
    mixed_all = matmul(normed, input_weight)
    query_all = both_ways(mixed_all[:, :, :feature_width] + query_bias)
    key_all = both_ways(mixed_all[:, :, feature_width:2 * feature_width])
    value_all = both_ways(mixed_all[:, :, 2 * feature_width:] + value_bias)
    query_all = query_all.reshape(groups, length, HEADS, head_size)
    key_all = key_all.reshape(groups, length, HEADS, head_size)
    value_all = value_all.reshape(groups, length, HEADS, head_size)
    scores = low_back(jnp.einsum('gqhe,gkhe->ghqk', query_all, key_all, precision=lax.Precision.HIGHEST) * score_scale)
    weights = jax.nn.softmax(scores, axis=-1)
    attended = jnp.einsum('ghqk,gkhe->gqhe', low(weights), value_all, precision=lax.Precision.HIGHEST)
    attended = both_ways(attended.reshape(groups, length, feature_width))
    branch = low_back(matmul(attended, output_weight) + output_bias)
    middle = images + branch
    normed_two = low(normalize(middle, second_gain, second_shift))
    hidden = low_back(matmul(normed_two, up_weight) + up_bias)
    active = low(jax.nn.gelu(hidden, approximate=False))
    return middle + matmul(active, down_weight) + down_bias

def reference(images, cotangent, first_gain, first_shift, input_weight, query_bias, value_bias, output_weight, output_bias, second_gain, second_shift, up_weight, up_bias, down_weight, down_bias):
    params = tuple((parameter.astype(jnp.float32) for parameter in (first_gain, first_shift, input_weight, query_bias, value_bias, output_weight, output_bias, second_gain, second_shift, up_weight, up_bias, down_weight, down_bias)))
    block_size = math.gcd(IMAGES, 4)
    block_count = IMAGES // block_size
    image_blocks = images.reshape(block_count, block_size, SEQ_LEN, D)
    cot_blocks = cotangent.reshape(block_count, block_size, SEQ_LEN, D)
    zero_sums = tuple((jnp.zeros(parameter.shape, jnp.float32) for parameter in params))

    def scan_step(totals, block_pair):
        inputs, cot_block = block_pair
        output, pullback = jax.vjp(forward, inputs.astype(jnp.float32), params)
        input_grad, param_grads = pullback(cot_block.astype(jnp.float32))
        totals = tuple((running + fresh for running, fresh in zip(totals, param_grads)))
        return (totals, (output.astype(jnp.bfloat16), input_grad))
    totals, (outputs, input_grads) = lax.scan(scan_step, zero_sums, (image_blocks, cot_blocks))
    first_gain_gradient, first_shift_gradient, input_weight_gradient, query_bias_gradient, value_bias_gradient, output_weight_gradient, output_bias_gradient, second_gain_gradient, second_shift_gradient, up_weight_gradient, up_bias_gradient, down_weight_gradient, down_bias_gradient = totals
    return (outputs.reshape(IMAGES, SEQ_LEN, D), input_grads.reshape(IMAGES, SEQ_LEN, D), first_gain_gradient, first_shift_gradient, input_weight_gradient, query_bias_gradient, value_bias_gradient, output_weight_gradient, output_bias_gradient, second_gain_gradient, second_shift_gradient, up_weight_gradient, up_bias_gradient, down_weight_gradient, down_bias_gradient)
```

```python
import functools
import math

import jax
import jax.numpy as jnp
from jax import lax
from jax.experimental import pallas as pl
from jax.experimental.pallas import tpu as pltpu
from jax.sharding import PartitionSpec as P

HEADS = 12


EPSILON = 1e-06


def normalize(features, scale_gain, shift_bias):
    row_mean = jnp.mean(features, axis=-1, keepdims=True)
    centred = features - row_mean
    row_var = jnp.mean(centred * centred, axis=-1, keepdims=True)
    return centred * lax.rsqrt(row_var + EPSILON) * scale_gain + shift_bias


def gelu_exact(features):
    return jax.nn.gelu(features, approximate=False)


def project(first_operand, second_operand):
    return jnp.einsum(
        "itk,kn->itn", first_operand, second_operand, preferred_element_type=jnp.float32
    )


def outer_sum(first_operand, second_operand):
    return jnp.einsum(
        "itk,itn->kn", first_operand, second_operand, preferred_element_type=jnp.float32
    )


def project_back(first_operand, second_operand):
    return jnp.einsum(
        "itn,kn->itk", first_operand, second_operand, preferred_element_type=jnp.float32
    )


def split_heads(features, head_count, head_group):
    image_count, token_count, feature_width = features.shape
    head_size = feature_width // head_count
    features = features.reshape(
        image_count, token_count, head_count // head_group, head_group, head_size
    )
    return features.transpose(2, 0, 3, 1, 4)


def join_heads(features):
    block_count, image_count, head_group, token_count, head_size = features.shape
    return features.transpose(1, 3, 0, 2, 4).reshape(
        image_count, token_count, block_count * head_group * head_size
    )


MESH = pl.DeviceIdType.MESH
LIMIT = 60000 * 1024


def meet_all(axes_list):
    barrier = pltpu.get_barrier_semaphore()
    for place in axes_list:
        pl.semaphore_signal(barrier, inc=1, device_id=place, device_id_type=MESH)
    pl.semaphore_wait(barrier, len(axes_list))


def plane_peers(flat, shards):
    for step in range(1, shards):
        peer = lax.rem(flat + step, shards)
        yield step, {"fsdp": lax.div(peer, 2), "seq": lax.rem(peer, 2)}


class Sender:
    def __init__(self, send_sem, recv_sem):
        self.send_sem, self.recv_sem, self.used = send_sem, recv_sem, 0

    def __call__(self, source, target, place):
        index = self.used
        self.used += 1
        return pltpu.make_async_remote_copy(
            src_ref=source,
            dst_ref=target,
            send_sem=self.send_sem.at[index],
            recv_sem=self.recv_sem.at[index],
            device_id=place,
            device_id_type=MESH,
        )


def gather_body(fsdp, count, *refs):
    weights, small, images = refs[:count], refs[count], refs[count + 1]
    outs = refs[count + 2 : 2 * count + 2]
    small_out, images_out = refs[2 * count + 2], refs[2 * count + 3]
    send_sem, recv_sem, local_sem = refs[2 * count + 4 :]
    ys = fsdp // 2
    me_f, x = lax.axis_index("fsdp"), lax.axis_index("seq")
    y, c = lax.div(me_f, 2), lax.rem(me_f, 2)
    flat = me_f * 2 + x
    shards = fsdp * 2
    make = Sender(send_sem, recv_sem)

    def slot(yy, cc, xx):
        return (yy * 2 + cc) * 2 + xx

    at_x = {"fsdp": me_f, "seq": 1 - x}
    at_core = {"fsdp": y * 2 + 1 - c, "seq": x}
    at_y = [{"fsdp": lax.rem(y + j, ys) * 2 + c, "seq": x} for j in range(1, ys)]
    from_y = [lax.rem(y + ys - j, ys) for j in range(1, ys)]
    meet_all([place for _, place in plane_peers(flat, shards)])
    sent, awaited, local = [], [], []

    def go(copy):
        copy.start()
        sent.append(copy)
        return copy

    for index, (source, target) in enumerate(zip(weights, outs)):
        keep = pltpu.make_async_copy(source, target.at[flat], local_sem.at[index])
        keep.start()
        local.append(keep)
    keep = pltpu.make_async_copy(small, small_out.at[flat], local_sem.at[count])
    keep.start()
    local.append(keep)
    for _, place in plane_peers(flat, shards):
        awaited.append(go(make(small, small_out.at[flat], place)))
    awaited.append(go(make(images, images_out, at_x)))
    first = []
    for source, target in zip(weights, outs):
        hand_x = go(make(source, target.at[flat], at_x))
        hand_y = [go(make(source, target.at[flat], place)) for place in at_y]
        awaited.append(go(make(source, target.at[flat], at_core)))
        first.append((hand_x, hand_y))
    second = []

    def relay_one(index):
        target = outs[index]
        half = weights[index].shape[1] // 2
        low, high = pl.ds(0, half), pl.ds(half, half)
        hand_x, hand_y = first[index]
        passed_y, passed_x = [], []
        hand_x.wait_recv()
        block = target.at[slot(y, c, 1 - x)]
        for place in at_y:
            part = block.at[:, low]
            passed_y.append(go(make(part, part, place)))
        awaited.append(go(make(block, block, at_core)))
        for yy, hand in zip(from_y, hand_y):
            hand.wait_recv()
            block = target.at[slot(yy, c, x)]
            part = block.at[:, high]
            passed_x.append(go(make(part, part, at_x)))
            awaited.append(go(make(block, block, at_core)))
        second.append((passed_y, passed_x))

    def relay_two(index):
        target = outs[index]
        half = weights[index].shape[1] // 2
        low, high = pl.ds(0, half), pl.ds(half, half)
        passed_y, passed_x = second[index]
        for yy, by_y, by_x in zip(from_y, passed_y, passed_x):
            block = target.at[slot(yy, c, 1 - x)]
            by_y.wait_recv()
            awaited.append(go(make(block.at[:, low], block.at[:, low], at_core)))
            by_x.wait_recv()
            awaited.append(go(make(block.at[:, high], block.at[:, high], at_core)))

    for index in range(count):
        relay_one(index)
        if index:
            relay_two(index - 1)
    relay_two(count - 1)
    for copy in awaited:
        copy.wait_recv()
    for copy in sent:
        copy.wait_send()
    for copy in local:
        copy.wait()


def gather_call(fsdp, weights, small, images):
    count = len(weights)
    shards = fsdp * 2
    ys = fsdp // 2
    copies = shards + count * (3 + 6 * (ys - 1) + 2)
    shapes = [jax.ShapeDtypeStruct((shards,) + w.shape, w.dtype) for w in weights]
    shapes.append(jax.ShapeDtypeStruct((shards,) + small.shape, small.dtype))
    shapes.append(jax.ShapeDtypeStruct(images.shape, images.dtype))
    return pl.pallas_call(
        lambda *refs: gather_body(fsdp, count, *refs),
        out_shape=shapes,
        in_specs=[pl.BlockSpec(memory_space=pltpu.VMEM)] * (count + 2),
        out_specs=[pl.BlockSpec(memory_space=pl.ANY)] * (count + 2),
        scratch_shapes=[
            pltpu.SemaphoreType.DMA((copies,)),
            pltpu.SemaphoreType.DMA((copies,)),
            pltpu.SemaphoreType.DMA((count + 1,)),
        ],
        compiler_params=pltpu.CompilerParams(
            collective_id=1, has_side_effects=True, vmem_limit_bytes=LIMIT
        ),
    )(*weights, small, images)


def reduce_body(fsdp, reps, groups, *refs):
    low = jnp.bfloat16
    parts, small = refs[:groups], refs[groups]
    outs, small_out = refs[groups + 1 : 2 * groups + 1], refs[2 * groups + 1]
    at = 2 * groups + 2
    got_core, got_a1, got_b1, got_a2, got_b2, whole, got_z, kept_z = [
        refs[at + i * groups : at + (i + 1) * groups] for i in range(8)
    ]
    small_got, small_sum, small_z, send_sem, recv_sem = refs[at + 8 * groups :]
    ys = fsdp // 2
    shards = fsdp * 2
    units = 8
    share = units // reps
    me_f, x, z = lax.axis_index("fsdp"), lax.axis_index("seq"), lax.axis_index("rep")
    y, c = lax.div(me_f, 2), lax.rem(me_f, 2)
    flat = me_f * 2 + x
    at_x = {"fsdp": me_f, "seq": 1 - x}
    at_core = {"fsdp": y * 2 + 1 - c, "seq": x}
    to_y = [lax.rem(y + j, ys) for j in range(1, ys)]
    at_y = [{"fsdp": yy * 2 + c, "seq": x} for yy in to_y]
    to_z = [lax.rem(z + d, reps) for d in range(1, reps)]
    at_z = [{"rep": zz} for zz in to_z]
    make = Sender(send_sem, recv_sem)
    sent = []

    def go(copy):
        copy.start()
        sent.append(copy)
        return copy

    meet_all([place for _, place in plane_peers(flat, shards)] + at_z)

    def loop(extent, step):
        lax.fori_loop(0, extent, lambda i, carry: (step(i), carry)[1], 0)

    core_hand = [go(make(part.at[:, :, 1 - c], got, at_core)) for part, got in zip(parts, got_core)]
    small_hand = []
    for step, place in plane_peers(flat, shards):
        peer = lax.rem(flat + step, shards)
        small_hand.append(go(make(small.at[peer], small_got.at[step - 1], place)))
    hands = {}

    def stage_core(g):
        core_hand[g].wait_recv()
        got, part = got_core[g], parts[g]

        def add(i):
            u, rest = lax.div(i, 2 * ys), lax.rem(i, 2 * ys)
            yy, xx = lax.div(rest, 2), lax.rem(rest, 2)
            got[u, yy, xx] = (
                got[u, yy, xx].astype(jnp.float32) + part[u, yy, c, xx].astype(jnp.float32)
            ).astype(low)

        loop(units * 2 * ys, add)
        a1 = go(make(got.at[pl.ds(0, 4), :, 1 - x], got_a1[g], at_x))
        b1 = [
            go(make(got.at[pl.ds(4, 4), yy], got_b1[g].at[j], place))
            for j, (yy, place) in enumerate(zip(to_y, at_y))
        ]
        hands[g] = [a1, b1]

    def stage_cross(g):
        a1, b1 = hands[g]
        got, from_x, from_y = got_core[g], got_a1[g], got_b1[g]
        a1.wait_recv()

        def add_a(i):
            u, yy = lax.div(i, ys), lax.rem(i, ys)
            got[u, yy, x] = (
                got[u, yy, x].astype(jnp.float32) + from_x[u, yy].astype(jnp.float32)
            ).astype(low)

        loop(4 * ys, add_a)
        a2 = [
            go(make(got.at[pl.ds(0, 4), yy, x], got_a2[g].at[j], place))
            for j, (yy, place) in enumerate(zip(to_y, at_y))
        ]
        for copy in b1:
            copy.wait_recv()

        def add_b(i):
            u, xx = lax.div(i, 2), lax.rem(i, 2)
            total = got[u + 4, y, xx].astype(jnp.float32)
            for j in range(ys - 1):
                total = total + from_y[j, u, xx].astype(jnp.float32)
            got[u + 4, y, xx] = total.astype(low)

        loop(8, add_b)
        b2 = go(make(got.at[pl.ds(4, 4), y, 1 - x], got_b2[g], at_x))
        hands[g] = [a2, b2]

    def stage_own(g):
        a2, b2 = hands[g]
        got, from_y, from_x, total_ref = got_core[g], got_a2[g], got_b2[g], whole[g]
        for copy in a2:
            copy.wait_recv()

        def add_a(u):
            total = got[u, y, x].astype(jnp.float32)
            for j in range(ys - 1):
                total = total + from_y[j, u].astype(jnp.float32)
            total_ref[u] = total.astype(low)

        loop(4, add_a)
        b2.wait_recv()

        def add_b(u):
            total_ref[u + 4] = (
                got[u + 4, y, x].astype(jnp.float32) + from_x[u].astype(jnp.float32)
            ).astype(low)

        loop(4, add_b)
        hands[g] = [
            go(make(total_ref.at[pl.ds(zz * share, share)], got_z[g].at[d], place))
            for d, (zz, place) in enumerate(zip(to_z, at_z))
        ]

    def stage_rep(g):
        for copy in hands[g]:
            copy.wait_recv()
        total_ref, from_z, kept = whole[g], got_z[g], kept_z[g]

        def add(u):
            total = total_ref[z * share + u].astype(jnp.float32)
            for d in range(reps - 1):
                total = total + from_z[d, u].astype(jnp.float32)
            kept[z * share + u] = total.astype(low)

        loop(share, add)
        mine = kept.at[pl.ds(z * share, share)]
        hands[g] = [go(make(mine, mine, place)) for place in at_z]

    def stage_end(g):
        for copy in hands[g]:
            copy.wait_recv()
        kept, out = kept_z[g], outs[g]

        def widen(u):
            out[u] = kept[u].astype(jnp.float32)

        loop(units, widen)

    for copy in small_hand:
        copy.wait_recv()
    total = small[flat]
    for step in range(shards - 1):
        total = total + small_got[step]
    small_sum[...] = total
    small_hand_z = [
        go(make(small_sum, small_z.at[d], place)) for d, place in enumerate(at_z)
    ]
    stages = (stage_core, stage_cross, stage_own, stage_rep, stage_end)
    for tick in range(groups + len(stages) - 1):
        for number, stage in enumerate(stages):
            g = tick - number
            if 0 <= g < groups:
                stage(g)
    for copy in small_hand_z:
        copy.wait_recv()
    total = small_sum[...]
    for d in range(reps - 1):
        total = total + small_z[d]
    small_out[...] = total
    for copy in sent:
        copy.wait_send()


def reduce_call(fsdp, reps, parts, small):
    groups = len(parts)
    shards, ys = fsdp * 2, fsdp // 2
    units, _, _, _, rows, width = parts[0].shape
    share = units // reps
    copies = (shards - 1) + (reps - 1) + groups * (1 + 1 + (ys - 1) * 2 + 1 + 2 * (reps - 1))
    low = jnp.bfloat16

    def many(*lead):
        return [pltpu.VMEM(lead + (rows, width), low)] * groups

    scratch = (
        many(units, ys, 2)
        + many(4, ys)
        + many(ys - 1, 4, 2)
        + many(ys - 1, 4)
        + many(4)
        + many(units)
        + many(reps - 1, share)
        + many(units)
        + [
            pltpu.VMEM((shards - 1,) + small.shape[1:], jnp.float32),
            pltpu.VMEM(small.shape[1:], jnp.float32),
            pltpu.VMEM((reps - 1,) + small.shape[1:], jnp.float32),
            pltpu.SemaphoreType.DMA((copies,)),
            pltpu.SemaphoreType.DMA((copies,)),
        ]
    )
    return pl.pallas_call(
        lambda *refs: reduce_body(fsdp, reps, groups, *refs),
        out_shape=[jax.ShapeDtypeStruct((units, rows, width), jnp.float32)] * groups
        + [jax.ShapeDtypeStruct(small.shape[1:], jnp.float32)],
        in_specs=[pl.BlockSpec(memory_space=pltpu.VMEM)] * (groups + 1),
        out_specs=[pl.BlockSpec(memory_space=pltpu.VMEM)] * (groups + 1),
        scratch_shapes=scratch,
        compiler_params=pltpu.CompilerParams(
            collective_id=2, has_side_effects=True, vmem_limit_bytes=LIMIT
        ),
    )(*parts, small)


def on_device(
    fsdp,
    reps,
    images,
    cotangent,
    first_gain,
    first_shift,
    input_weight,
    query_bias,
    value_bias,
    output_weight,
    output_bias,
    second_gain,
    second_shift,
    up_weight,
    up_bias,
    down_weight,
    down_bias,
):
    feature_width = images.shape[2]
    score_scale = 1.0 / math.sqrt(feature_width // HEADS)

    def attend_block(operands):
        query_block, key_block, value_block = operands
        scores = (
            jnp.einsum(
                "ihqe,ihke->ihqk", query_block, key_block, preferred_element_type=jnp.float32
            )
            * score_scale
        )
        row_peak = jnp.max(scores, axis=-1, keepdims=True)
        shifted = jnp.exp(scores - row_peak)
        row_total = jnp.sum(shifted, axis=-1, keepdims=True)
        weights_low = (shifted / row_total).astype(jnp.bfloat16)
        result = jnp.einsum(
            "ihqk,ihke->ihqe", weights_low, value_block, preferred_element_type=jnp.float32
        )
        return (result, row_peak[..., 0] + jnp.log(row_total[..., 0]))

    def attend_back(operands):
        query_block, key_block, value_block, grad_block, logsum = operands
        scores = (
            jnp.einsum(
                "ihqe,ihke->ihqk", query_block, key_block, preferred_element_type=jnp.float32
            )
            * score_scale
        )
        weights_full = jnp.exp(scores - logsum[..., None])
        grad_weights = jnp.einsum(
            "ihqe,ihke->ihqk", grad_block, value_block, preferred_element_type=jnp.float32
        )
        inner = jnp.sum(weights_full * grad_weights, axis=-1, keepdims=True)
        grad_scores = (weights_full * (grad_weights - inner)).astype(jnp.bfloat16)
        grad_query = (
            jnp.einsum(
                "ihqk,ihke->ihqe", grad_scores, key_block, preferred_element_type=jnp.float32
            )
            * score_scale
        )
        grad_key = (
            jnp.einsum(
                "ihqk,ihqe->ihke", grad_scores, query_block, preferred_element_type=jnp.float32
            )
            * score_scale
        )
        grad_value = jnp.einsum(
            "ihqk,ihqe->ihke",
            weights_full.astype(jnp.bfloat16),
            grad_block,
            preferred_element_type=jnp.float32,
        )
        return (grad_query, grad_key, grad_value)

    pieces = (
        first_gain, first_shift, query_bias, value_bias, output_bias,
        second_gain, second_shift, down_bias, up_bias,
    )
    shards = fsdp * 2
    small = jnp.concatenate([p.astype(jnp.float32) for p in pieces])[None]
    fulls = gather_call(
        fsdp, (input_weight, output_weight, up_weight, down_weight), small, images[0]
    )
    input_full, output_full, up_full, down_full = [
        w.reshape(-1, w.shape[-1]) for w in fulls[:4]
    ]
    images_other = fulls[5]
    rows = first_gain.shape[0]
    small_full = fulls[4].reshape(shards, -1)
    eight = small_full[:, : 8 * rows].reshape(shards, 8, rows).transpose(1, 0, 2).reshape(8, -1)
    gain_one, shift_one, query_add, value_add, output_add, gain_two, shift_two, down_add = [
        eight[i] for i in range(8)
    ]
    up_add = small_full[:, 8 * rows :].reshape(-1)

    inputs = images.astype(jnp.float32)
    normed_one = normalize(inputs, gain_one, shift_one).astype(jnp.bfloat16)
    normed_other = normalize(
        images_other[None].astype(jnp.float32), gain_one, shift_one
    ).astype(jnp.bfloat16)
    normed_all = jnp.concatenate([normed_one, normed_other], axis=1)
    head_local = HEADS
    head_group = math.gcd(head_local, 4)
    width = feature_width
    tokens = images.shape[1]
    query_local = (project(normed_one, input_full[:, :width]) + query_add).astype(jnp.bfloat16)
    mixed_kv = project(normed_all, input_full[:, width:])
    keys_all = mixed_kv[:, :, :width].astype(jnp.bfloat16)
    values_all = (mixed_kv[:, :, width:] + value_add).astype(jnp.bfloat16)
    query_heads = split_heads(query_local, head_local, head_group)
    key_heads = split_heads(keys_all, head_local, head_group)
    value_heads = split_heads(values_all, head_local, head_group)
    attended_heads, logsum = lax.map(attend_block, (query_heads, key_heads, value_heads))
    attended_local = join_heads(attended_heads).astype(jnp.bfloat16)
    middle = inputs + project(attended_local, output_full) + output_add
    normed_two = normalize(middle, gain_two, shift_two).astype(jnp.bfloat16)
    hidden = project(normed_two, up_full) + up_add
    active = gelu_exact(hidden).astype(jnp.bfloat16)
    branch_sum = project(active, down_full)
    layer_out = (middle + branch_sum + down_add).astype(jnp.bfloat16)

    grad_down = outer_sum(active, cotangent).astype(jnp.bfloat16)
    grad_down_bias = jnp.sum(cotangent, axis=(0, 1), dtype=jnp.float32)
    grad_active = project_back(cotangent, down_full)
    gelu_value, gelu_pull = jax.vjp(gelu_exact, hidden)
    grad_hidden = gelu_pull(grad_active)[0].astype(jnp.bfloat16)
    grad_up_bias = jnp.sum(grad_hidden, axis=(0, 1), dtype=jnp.float32)
    grad_up = outer_sum(normed_two, grad_hidden).astype(jnp.bfloat16)
    grad_normed_two = project_back(grad_hidden, up_full)
    norm_value, second_pull = jax.vjp(normalize, middle, gain_two, shift_two)
    grad_middle_norm, grad_gain_two, grad_shift_two = second_pull(grad_normed_two)
    grad_middle = cotangent.astype(jnp.float32) + grad_middle_norm
    grad_branch = grad_middle.astype(jnp.bfloat16)
    grad_out_bias = jnp.sum(grad_branch, axis=(0, 1), dtype=jnp.float32)
    grad_weight_out = outer_sum(attended_local, grad_branch).astype(jnp.bfloat16)
    grad_attended = project_back(grad_branch, output_full).astype(jnp.bfloat16)
    grad_heads = split_heads(grad_attended, head_local, head_group)
    query_parts, key_parts, value_parts = lax.map(
        attend_back, (query_heads, key_heads, value_heads, grad_heads, logsum)
    )
    grad_query = join_heads(query_parts).astype(jnp.bfloat16)
    grad_keys_part = join_heads(key_parts)
    grad_values_part = join_heads(value_parts)
    grad_query_bias = jnp.sum(grad_query, axis=(0, 1), dtype=jnp.float32)
    grad_value_bias = jnp.sum(grad_values_part, axis=(0, 1), dtype=jnp.float32)
    grad_kv = jnp.concatenate([grad_keys_part, grad_values_part], axis=-1).astype(jnp.bfloat16)
    grad_normed_kv = project_back(grad_kv, input_full[:, width:])
    to_other = grad_normed_kv[:, tokens:].astype(jnp.bfloat16)
    from_other = lax.ppermute(to_other, "seq", [(0, 1), (1, 0)])
    grad_weight_q = outer_sum(normed_one, grad_query).astype(jnp.bfloat16)
    grad_weight_kv = outer_sum(normed_all, grad_kv).astype(jnp.bfloat16)
    grad_normed_one = (
        grad_normed_kv[:, :tokens]
        + project_back(grad_query, input_full[:, :width])
        + from_other.astype(jnp.float32)
    )
    first_value, first_pull = jax.vjp(normalize, inputs, gain_one, shift_one)
    grad_inputs_norm, grad_gain_one, grad_shift_one = first_pull(grad_normed_one)
    input_gradient = grad_middle + grad_inputs_norm

    ys = fsdp // 2
    chunk = width // 2

    def columns(grad):
        return grad.reshape(ys, 2, 2, rows, -1, chunk).transpose(4, 0, 1, 2, 3, 5)

    down_part = (
        grad_down.reshape(ys, 2, 2, 4, rows, 2, chunk)
        .transpose(3, 5, 0, 1, 2, 4, 6)
        .reshape(8, ys, 2, 2, rows, chunk)
    )
    up_part = columns(grad_up)
    rest_part = jnp.concatenate(
        [columns(grad_weight_q), columns(grad_weight_kv), columns(grad_weight_out)], axis=0
    )
    eight_grad = jnp.stack(
        [
            grad_gain_one, grad_shift_one, grad_query_bias, grad_value_bias,
            grad_out_bias, grad_gain_two, grad_shift_two, grad_down_bias,
        ]
    ).reshape(8, shards, rows).transpose(1, 0, 2).reshape(shards, 8 * rows)
    small_grad = jnp.concatenate([eight_grad, grad_up_bias.reshape(shards, -1)], axis=1)
    down_sum, up_sum, rest_sum, small_sum = reduce_call(
        fsdp, reps, (down_part, up_part, rest_part), small_grad[:, None]
    )

    def rows_of(summed):
        return summed.transpose(1, 0, 2).reshape(rows, -1)

    down_own = (
        down_sum.reshape(4, 2, rows, chunk).transpose(0, 2, 1, 3).reshape(4 * rows, width)
    )
    eight_own = small_sum[0, : 8 * rows].reshape(8, rows)
    return (
        layer_out,
        input_gradient,
        eight_own[0],
        eight_own[1],
        rows_of(rest_sum[:6]),
        eight_own[2],
        eight_own[3],
        rows_of(rest_sum[6:]),
        eight_own[4],
        eight_own[5],
        eight_own[6],
        rows_of(up_sum),
        small_sum[0, 8 * rows :],
        down_own,
        eight_own[7],
    )


def solution(mesh):
    placed = (
        P(("rep", "fsdp"), "seq", None),
        P(("rep", "fsdp"), "seq", None),
        P(("fsdp", "seq")),
        P(("fsdp", "seq")),
        P(("fsdp", "seq"), None),
        P(("fsdp", "seq")),
        P(("fsdp", "seq")),
        P(("fsdp", "seq"), None),
        P(("fsdp", "seq")),
        P(("fsdp", "seq")),
        P(("fsdp", "seq")),
        P(("fsdp", "seq"), None),
        P(("fsdp", "seq")),
        P(("fsdp", "seq"), None),
        P(("fsdp", "seq")),
    )
    return jax.shard_map(
        functools.partial(on_device, mesh.shape["fsdp"], mesh.shape["rep"]),
        mesh=mesh,
        in_specs=placed,
        out_specs=(
            P(("rep", "fsdp"), "seq", None),
            P(("rep", "fsdp"), "seq", None),
            P(("fsdp", "seq")),
            P(("fsdp", "seq")),
            P(("fsdp", "seq"), None),
            P(("fsdp", "seq")),
            P(("fsdp", "seq")),
            P(("fsdp", "seq"), None),
            P(("fsdp", "seq")),
            P(("fsdp", "seq")),
            P(("fsdp", "seq")),
            P(("fsdp", "seq"), None),
            P(("fsdp", "seq")),
            P(("fsdp", "seq"), None),
            P(("fsdp", "seq")),
        ),
        check_vma=False,
    )
```

```python
import functools
import math

import jax
import jax.numpy as jnp
from jax import lax
from jax.experimental import pallas as pl
from jax.experimental.pallas import tpu as pltpu
from jax.sharding import PartitionSpec as P

HEADS = 12


EPSILON = 1e-06


def normalize(features, scale_gain, shift_bias):
    row_mean = jnp.mean(features, axis=-1, keepdims=True)
    centred = features - row_mean
    row_var = jnp.mean(centred * centred, axis=-1, keepdims=True)
    return centred * lax.rsqrt(row_var + EPSILON) * scale_gain + shift_bias


def gelu_exact(features):
    return jax.nn.gelu(features, approximate=False)


def project(first_operand, second_operand):
    return jnp.einsum(
        "itk,kn->itn", first_operand, second_operand, preferred_element_type=jnp.float32
    )


def project_back(first_operand, second_operand):
    return jnp.einsum(
        "itn,kn->itk", first_operand, second_operand, preferred_element_type=jnp.float32
    )


MESH = pl.DeviceIdType.MESH
LIMIT = 60000 * 1024


def meet_all(axes_list):
    barrier = pltpu.get_barrier_semaphore()
    for place in axes_list:
        pl.semaphore_signal(barrier, inc=1, device_id=place, device_id_type=MESH)
    pl.semaphore_wait(barrier, len(axes_list))


def plane_peers(flat, shards):
    for step in range(1, shards):
        peer = lax.rem(flat + step, shards)
        yield step, {"fsdp": lax.div(peer, 2), "seq": lax.rem(peer, 2)}


class Sender:
    def __init__(self, send_sem, recv_sem):
        self.send_sem, self.recv_sem, self.used = send_sem, recv_sem, 0

    def __call__(self, source, target, place):
        index = self.used
        self.used += 1
        return pltpu.make_async_remote_copy(
            src_ref=source,
            dst_ref=target,
            send_sem=self.send_sem.at[index],
            recv_sem=self.recv_sem.at[index],
            device_id=place,
            device_id_type=MESH,
        )


def gather_body(fsdp, count, *refs):
    weights, small, images = refs[:count], refs[count], refs[count + 1]
    outs = refs[count + 2 : 2 * count + 2]
    small_out, images_out = refs[2 * count + 2], refs[2 * count + 3]
    send_sem, recv_sem, local_sem = refs[2 * count + 4 :]
    ys = fsdp // 2
    me_f, x = lax.axis_index("fsdp"), lax.axis_index("seq")
    y, c = lax.div(me_f, 2), lax.rem(me_f, 2)
    flat = me_f * 2 + x
    shards = fsdp * 2
    make = Sender(send_sem, recv_sem)

    def slot(yy, cc, xx):
        return (yy * 2 + cc) * 2 + xx

    at_x = {"fsdp": me_f, "seq": 1 - x}
    at_core = {"fsdp": y * 2 + 1 - c, "seq": x}
    at_y = [{"fsdp": lax.rem(y + j, ys) * 2 + c, "seq": x} for j in range(1, ys)]
    from_y = [lax.rem(y + ys - j, ys) for j in range(1, ys)]
    meet_all([place for _, place in plane_peers(flat, shards)])
    sent, awaited, local = [], [], []

    def go(copy):
        copy.start()
        sent.append(copy)
        return copy

    for index, (source, target) in enumerate(zip(weights, outs)):
        keep = pltpu.make_async_copy(source, target.at[flat], local_sem.at[index])
        keep.start()
        local.append(keep)
    keep = pltpu.make_async_copy(small, small_out.at[flat], local_sem.at[count])
    keep.start()
    local.append(keep)
    for _, place in plane_peers(flat, shards):
        awaited.append(go(make(small, small_out.at[flat], place)))
    awaited.append(go(make(images, images_out, at_x)))
    first = []
    for source, target in zip(weights, outs):
        hand_x = go(make(source, target.at[flat], at_x))
        hand_y = [go(make(source, target.at[flat], place)) for place in at_y]
        awaited.append(go(make(source, target.at[flat], at_core)))
        first.append((hand_x, hand_y))
    second = []

    def relay_one(index):
        target = outs[index]
        half = weights[index].shape[1] // 2
        low, high = pl.ds(0, half), pl.ds(half, half)
        hand_x, hand_y = first[index]
        passed_y, passed_x = [], []
        hand_x.wait_recv()
        block = target.at[slot(y, c, 1 - x)]
        for place in at_y:
            part = block.at[:, low]
            passed_y.append(go(make(part, part, place)))
        awaited.append(go(make(block, block, at_core)))
        for yy, hand in zip(from_y, hand_y):
            hand.wait_recv()
            block = target.at[slot(yy, c, x)]
            part = block.at[:, high]
            passed_x.append(go(make(part, part, at_x)))
            awaited.append(go(make(block, block, at_core)))
        second.append((passed_y, passed_x))

    def relay_two(index):
        target = outs[index]
        half = weights[index].shape[1] // 2
        low, high = pl.ds(0, half), pl.ds(half, half)
        passed_y, passed_x = second[index]
        for yy, by_y, by_x in zip(from_y, passed_y, passed_x):
            block = target.at[slot(yy, c, 1 - x)]
            by_y.wait_recv()
            awaited.append(go(make(block.at[:, low], block.at[:, low], at_core)))
            by_x.wait_recv()
            awaited.append(go(make(block.at[:, high], block.at[:, high], at_core)))

    for index in range(count):
        relay_one(index)
        if index:
            relay_two(index - 1)
    relay_two(count - 1)
    for copy in awaited:
        copy.wait_recv()
    for copy in sent:
        copy.wait_send()
    for copy in local:
        copy.wait()


def gather_call(fsdp, weights, small, images):
    count = len(weights)
    shards = fsdp * 2
    ys = fsdp // 2
    copies = shards + count * (3 + 6 * (ys - 1) + 2)
    shapes = [jax.ShapeDtypeStruct((shards,) + w.shape, w.dtype) for w in weights]
    shapes.append(jax.ShapeDtypeStruct((shards,) + small.shape, small.dtype))
    shapes.append(jax.ShapeDtypeStruct(images.shape, images.dtype))
    return pl.pallas_call(
        lambda *refs: gather_body(fsdp, count, *refs),
        out_shape=shapes,
        in_specs=[pl.BlockSpec(memory_space=pltpu.VMEM)] * (count + 2),
        out_specs=[pl.BlockSpec(memory_space=pl.ANY)] * (count + 2),
        scratch_shapes=[
            pltpu.SemaphoreType.DMA((copies,)),
            pltpu.SemaphoreType.DMA((copies,)),
            pltpu.SemaphoreType.DMA((count + 1,)),
        ],
        compiler_params=pltpu.CompilerParams(
            collective_id=1, has_side_effects=True, vmem_limit_bytes=LIMIT
        ),
    )(*weights, small, images)


def reduce_body(fsdp, reps, groups, *refs):
    low = jnp.bfloat16
    (
        active, cot, normed_two, grad_hidden, normed_all,
        grad_query, grad_keys, grad_values, attended, grad_branch, small,
    ) = refs[:11]
    outs, small_out = refs[11 : 11 + groups], refs[11 + groups]
    at = 12 + groups
    got_core, got_a1, got_b1, got_a2, got_b2, whole, got_z, kept_z, parts = [
        refs[at + i * groups : at + (i + 1) * groups] for i in range(9)
    ]
    small_got, small_sum, small_z, send_sem, recv_sem = refs[at + 9 * groups :]
    ys = fsdp // 2
    shards = fsdp * 2
    units = 8
    share = units // reps
    me_f, x, z = lax.axis_index("fsdp"), lax.axis_index("seq"), lax.axis_index("rep")
    y, c = lax.div(me_f, 2), lax.rem(me_f, 2)
    flat = me_f * 2 + x
    at_x = {"fsdp": me_f, "seq": 1 - x}
    at_core = {"fsdp": y * 2 + 1 - c, "seq": x}
    to_y = [lax.rem(y + j, ys) for j in range(1, ys)]
    at_y = [{"fsdp": yy * 2 + c, "seq": x} for yy in to_y]
    to_z = [lax.rem(z + d, reps) for d in range(1, reps)]
    at_z = [{"rep": zz} for zz in to_z]
    make = Sender(send_sem, recv_sem)
    sent = []

    def go(copy):
        copy.start()
        sent.append(copy)
        return copy

    meet_all([place for _, place in plane_peers(flat, shards)] + at_z)

    def loop(extent, step):
        lax.fori_loop(0, extent, lambda i, carry: (step(i), carry)[1], 0)

    core_hand = {}
    tokens = cot.shape[0]
    rows, chunk = parts[0].shape[-2:]

    def outer(left, right):
        return lax.dot_general(
            left, right, (((0,), (0,)), ((), ())), preferred_element_type=jnp.float32
        )

    def columns(part, first, left, right):
        def one(u):
            start = pl.multiple_of(u * chunk, 128)
            total = outer(left[...], right[:, pl.ds(start, chunk)])
            part[first + u] = total.reshape(ys, 2, 2, rows, chunk).astype(low)

        loop(right.shape[1] // chunk, one)

    def stage_grads(g):
        part = parts[g]
        if g == 0:
            width = cot.shape[1]
            per = width // (4 * rows)

            def one(block):
                start = pl.multiple_of(block * width, 128)
                total = outer(active[:, pl.ds(start, width)], cot[...])
                for near in range(per):
                    owner = block * per + near
                    yy, cc, xx = lax.div(owner, 4), lax.rem(lax.div(owner, 2), 2), lax.rem(owner, 2)
                    for i in range(4):
                        top = (near * 4 + i) * rows
                        for j in range(2):
                            part[i * 2 + j, yy, cc, xx] = total[
                                top : top + rows, j * chunk : (j + 1) * chunk
                            ].astype(low)

            loop(active.shape[1] // width, one)
        elif g == 1:
            columns(part, 0, normed_two, grad_hidden)
        else:
            columns(part, 0, normed_all.at[pl.ds(0, tokens)], grad_query)
            columns(part, 2, normed_all, grad_keys)
            columns(part, 4, normed_all, grad_values)
            columns(part, 6, attended, grad_branch)
        core_hand[g] = go(make(part.at[:, :, 1 - c], got_core[g], at_core))

    small_hand = []
    for step, place in plane_peers(flat, shards):
        peer = lax.rem(flat + step, shards)
        small_hand.append(go(make(small.at[peer], small_got.at[step - 1], place)))
    hands = {}

    def stage_core(g):
        core_hand[g].wait_recv()
        got, part = got_core[g], parts[g]

        def add(i):
            u, rest = lax.div(i, 2 * ys), lax.rem(i, 2 * ys)
            yy, xx = lax.div(rest, 2), lax.rem(rest, 2)
            got[u, yy, xx] = got[u, yy, xx] + part[u, yy, c, xx]

        loop(units * 2 * ys, add)
        a1 = go(make(got.at[pl.ds(0, 4), :, 1 - x], got_a1[g], at_x))
        b1 = [
            go(make(got.at[pl.ds(4, 4), yy], got_b1[g].at[j], place))
            for j, (yy, place) in enumerate(zip(to_y, at_y))
        ]
        hands[g] = [a1, b1]

    def stage_cross(g):
        a1, b1 = hands[g]
        got, from_x, from_y = got_core[g], got_a1[g], got_b1[g]
        a1.wait_recv()

        def add_a(i):
            u, yy = lax.div(i, ys), lax.rem(i, ys)
            got[u, yy, x] = got[u, yy, x] + from_x[u, yy]

        loop(4 * ys, add_a)
        a2 = [
            go(make(got.at[pl.ds(0, 4), yy, x], got_a2[g].at[j], place))
            for j, (yy, place) in enumerate(zip(to_y, at_y))
        ]
        for copy in b1:
            copy.wait_recv()

        def add_b(i):
            u, xx = lax.div(i, 2), lax.rem(i, 2)
            total = got[u + 4, y, xx].astype(jnp.float32)
            for j in range(ys - 1):
                total = total + from_y[j, u, xx].astype(jnp.float32)
            got[u + 4, y, xx] = total.astype(low)

        loop(8, add_b)
        b2 = go(make(got.at[pl.ds(4, 4), y, 1 - x], got_b2[g], at_x))
        hands[g] = [a2, b2]

    def stage_own(g):
        a2, b2 = hands[g]
        got, from_y, from_x, total_ref = got_core[g], got_a2[g], got_b2[g], whole[g]
        for copy in a2:
            copy.wait_recv()

        def add_a(u):
            total = got[u, y, x].astype(jnp.float32)
            for j in range(ys - 1):
                total = total + from_y[j, u].astype(jnp.float32)
            total_ref[u] = total.astype(low)

        loop(4, add_a)
        b2.wait_recv()

        def add_b(u):
            total_ref[u + 4] = got[u + 4, y, x] + from_x[u]

        loop(4, add_b)
        hands[g] = [
            go(make(total_ref.at[pl.ds(zz * share, share)], got_z[g].at[d], place))
            for d, (zz, place) in enumerate(zip(to_z, at_z))
        ]

    def stage_rep(g):
        for copy in hands[g]:
            copy.wait_recv()
        total_ref, from_z, kept = whole[g], got_z[g], kept_z[g]

        def add(u):
            total = total_ref[z * share + u].astype(jnp.float32)
            for d in range(reps - 1):
                total = total + from_z[d, u].astype(jnp.float32)
            kept[z * share + u] = total.astype(low)

        loop(share, add)
        mine = kept.at[pl.ds(z * share, share)]
        hands[g] = [go(make(mine, mine, place)) for place in at_z]

    def stage_end(g):
        for copy in hands[g]:
            copy.wait_recv()
        kept, out = kept_z[g], outs[g]

        def widen(u):
            out[u] = kept[u].astype(jnp.float32)

        loop(units, widen)

    stages = (stage_grads, stage_core, stage_cross, stage_own, stage_rep, stage_end)
    for tick in range(groups + len(stages) - 1):
        if tick == groups:
            for copy in small_hand:
                copy.wait_recv()
            total = small[flat]
            for step in range(shards - 1):
                total = total + small_got[step]
            small_sum[...] = total
            small_hand_z = [
                go(make(small_sum, small_z.at[d], place)) for d, place in enumerate(at_z)
            ]
        for number, stage in enumerate(stages):
            g = tick - number
            if 0 <= g < groups:
                stage(g)
    for copy in small_hand_z:
        copy.wait_recv()
    total = small_sum[...]
    for d in range(reps - 1):
        total = total + small_z[d]
    small_out[...] = total
    for copy in sent:
        copy.wait_send()


def reduce_call(fsdp, reps, operands, small):
    groups = 3
    shards, ys = fsdp * 2, fsdp // 2
    units, rows, width = 8, operands[1].shape[1] // shards, operands[1].shape[1] // 2
    share = units // reps
    copies = (shards - 1) + (reps - 1) + groups * (1 + 1 + (ys - 1) * 2 + 1 + 2 * (reps - 1))
    low = jnp.bfloat16

    def many(*lead):
        return [pltpu.VMEM(lead + (rows, width), low)] * groups

    scratch = (
        many(units, ys, 2)
        + many(4, ys)
        + many(ys - 1, 4, 2)
        + many(ys - 1, 4)
        + many(4)
        + many(units)
        + many(reps - 1, share)
        + many(units)
        + many(units, ys, 2, 2)
        + [
            pltpu.VMEM((shards - 1,) + small.shape[1:], jnp.float32),
            pltpu.VMEM(small.shape[1:], jnp.float32),
            pltpu.VMEM((reps - 1,) + small.shape[1:], jnp.float32),
            pltpu.SemaphoreType.DMA((copies,)),
            pltpu.SemaphoreType.DMA((copies,)),
        ]
    )
    return pl.pallas_call(
        lambda *refs: reduce_body(fsdp, reps, groups, *refs),
        out_shape=[jax.ShapeDtypeStruct((units, rows, width), jnp.float32)] * groups
        + [jax.ShapeDtypeStruct(small.shape[1:], jnp.float32)],
        in_specs=[pl.BlockSpec(memory_space=pltpu.VMEM)] * 11,
        out_specs=[pl.BlockSpec(memory_space=pltpu.VMEM)] * (groups + 1),
        scratch_shapes=scratch,
        compiler_params=pltpu.CompilerParams(
            collective_id=2, has_side_effects=True, vmem_limit_bytes=LIMIT
        ),
    )(*operands, small)


def attend_body(scale, head, query, keys, values, out, logsum):
    for part in range(2):
        at = slice(part * head, (part + 1) * head)
        scores = scale * lax.dot_general(
            query[:, at], keys[:, at], (((1,), (1,)), ((), ())),
            preferred_element_type=jnp.float32,
        )
        peak = jnp.max(scores, axis=-1, keepdims=True)
        shifted = jnp.exp(scores - peak)
        total = jnp.sum(shifted, axis=-1, keepdims=True)
        low = (shifted * (1.0 / total)).astype(jnp.bfloat16)
        out[:, at] = jnp.dot(
            low, values[:, at], preferred_element_type=jnp.float32
        ).astype(jnp.bfloat16)
        logsum[0, :, part : part + 1] = peak + jnp.log(total)


def attend_call(query, keys, values):
    tokens, width = query.shape
    head = width // HEADS
    pairs = HEADS // 2
    mine = pl.BlockSpec((tokens, 2 * head), lambda i: (0, i))
    full = pl.BlockSpec((keys.shape[0], 2 * head), lambda i: (0, i))
    return pl.pallas_call(
        functools.partial(attend_body, 1.0 / math.sqrt(head), head),
        grid=(pairs,),
        out_shape=[
            jax.ShapeDtypeStruct((tokens, width), jnp.bfloat16),
            jax.ShapeDtypeStruct((pairs, tokens, 2), jnp.float32),
        ],
        in_specs=[mine, full, full],
        out_specs=[mine, pl.BlockSpec((1, tokens, 2), lambda i: (i, 0, 0))],
    )(query, keys, values)


def attend_back_body(
    scale, head, query, keys, values, grad, logsum, grad_query, grad_keys, grad_values
):
    low = jnp.bfloat16

    def dot(left, right, left_dim, right_dim):
        return lax.dot_general(
            left, right, (((left_dim,), (right_dim,)), ((), ())),
            preferred_element_type=jnp.float32,
        )

    for part in range(2):
        at = slice(part * head, (part + 1) * head)
        q, k, v, g = query[:, at], keys[:, at], values[:, at], grad[:, at]
        weights = jnp.exp(scale * dot(q, k, 1, 1) - logsum[0, :, part : part + 1])
        grad_weights = dot(g, v, 1, 1)
        inner = jnp.sum(weights * grad_weights, axis=-1, keepdims=True)
        grad_scores = (weights * (grad_weights - inner)).astype(low)
        grad_query[:, at] = (scale * dot(grad_scores, k, 1, 0)).astype(low)
        grad_keys[:, at] = (scale * dot(grad_scores, q, 0, 0)).astype(low)
        grad_values[:, at] = dot(weights.astype(low), g, 0, 0).astype(low)


def attend_back_call(query, keys, values, grad, logsum):
    tokens, width = query.shape
    head = width // HEADS
    pairs = HEADS // 2
    mine = pl.BlockSpec((tokens, 2 * head), lambda i: (0, i))
    full = pl.BlockSpec((keys.shape[0], 2 * head), lambda i: (0, i))
    return pl.pallas_call(
        functools.partial(attend_back_body, 1.0 / math.sqrt(head), head),
        grid=(pairs,),
        out_shape=[
            jax.ShapeDtypeStruct(query.shape, jnp.bfloat16),
            jax.ShapeDtypeStruct(keys.shape, jnp.bfloat16),
            jax.ShapeDtypeStruct(keys.shape, jnp.bfloat16),
        ],
        in_specs=[mine, full, full, mine, pl.BlockSpec((1, tokens, 2), lambda i: (i, 0, 0))],
        out_specs=[mine, full, full],
    )(query, keys, values, grad, logsum)


def on_device(
    fsdp,
    reps,
    images,
    cotangent,
    first_gain,
    first_shift,
    input_weight,
    query_bias,
    value_bias,
    output_weight,
    output_bias,
    second_gain,
    second_shift,
    up_weight,
    up_bias,
    down_weight,
    down_bias,
):
    feature_width = images.shape[2]
    pieces = (
        first_gain, first_shift, query_bias, value_bias, output_bias,
        second_gain, second_shift, down_bias, up_bias,
    )
    shards = fsdp * 2
    small = jnp.concatenate([p.astype(jnp.float32) for p in pieces])[None]
    fulls = gather_call(
        fsdp, (input_weight, output_weight, up_weight, down_weight), small, images[0]
    )
    input_full, output_full, up_full, down_full = [
        w.reshape(-1, w.shape[-1]) for w in fulls[:4]
    ]
    images_other = fulls[5]
    rows = first_gain.shape[0]
    small_full = fulls[4].reshape(shards, -1)
    eight = small_full[:, : 8 * rows].reshape(shards, 8, rows).transpose(1, 0, 2).reshape(8, -1)
    gain_one, shift_one, query_add, value_add, output_add, gain_two, shift_two, down_add = [
        eight[i] for i in range(8)
    ]
    up_add = small_full[:, 8 * rows :].reshape(-1)

    inputs = images.astype(jnp.float32)
    normed_one = normalize(inputs, gain_one, shift_one).astype(jnp.bfloat16)
    normed_other = normalize(
        images_other[None].astype(jnp.float32), gain_one, shift_one
    ).astype(jnp.bfloat16)
    normed_all = jnp.concatenate([normed_one, normed_other], axis=1)
    width = feature_width
    tokens = images.shape[1]
    query_local = (project(normed_one, input_full[:, :width]) + query_add).astype(jnp.bfloat16)
    mixed_kv = project(normed_all, input_full[:, width:])
    keys_all = mixed_kv[:, :, :width].astype(jnp.bfloat16)
    values_all = (mixed_kv[:, :, width:] + value_add).astype(jnp.bfloat16)
    attended, logsum = attend_call(query_local[0], keys_all[0], values_all[0])
    attended_local = attended[None]
    middle = inputs + project(attended_local, output_full) + output_add
    normed_two = normalize(middle, gain_two, shift_two).astype(jnp.bfloat16)
    hidden = project(normed_two, up_full) + up_add
    active = gelu_exact(hidden).astype(jnp.bfloat16)
    branch_sum = project(active, down_full)
    layer_out = (middle + branch_sum + down_add).astype(jnp.bfloat16)

    grad_down_bias = jnp.sum(cotangent, axis=(0, 1), dtype=jnp.float32)
    grad_active = project_back(cotangent, down_full)
    gelu_value, gelu_pull = jax.vjp(gelu_exact, hidden)
    grad_hidden = gelu_pull(grad_active)[0].astype(jnp.bfloat16)
    grad_up_bias = jnp.sum(grad_hidden, axis=(0, 1), dtype=jnp.float32)
    grad_normed_two = project_back(grad_hidden, up_full)
    norm_value, second_pull = jax.vjp(normalize, middle, gain_two, shift_two)
    grad_middle_norm, grad_gain_two, grad_shift_two = second_pull(grad_normed_two)
    grad_middle = cotangent.astype(jnp.float32) + grad_middle_norm
    grad_branch = grad_middle.astype(jnp.bfloat16)
    grad_out_bias = jnp.sum(grad_branch, axis=(0, 1), dtype=jnp.float32)
    grad_attended = project_back(grad_branch, output_full).astype(jnp.bfloat16)
    grad_query, grad_keys, grad_values = attend_back_call(
        query_local[0], keys_all[0], values_all[0], grad_attended[0], logsum
    )
    grad_query_bias = jnp.sum(grad_query, axis=0, dtype=jnp.float32)
    grad_value_bias = jnp.sum(grad_values, axis=0, dtype=jnp.float32)
    grad_normed_kv = project_back(grad_keys[None], input_full[:, width : 2 * width])
    grad_normed_kv = grad_normed_kv + project_back(grad_values[None], input_full[:, 2 * width :])
    to_other = grad_normed_kv[:, tokens:].astype(jnp.bfloat16)
    from_other = lax.ppermute(to_other, "seq", [(0, 1), (1, 0)])
    grad_normed_one = (
        grad_normed_kv[:, :tokens]
        + project_back(grad_query[None], input_full[:, :width])
        + from_other.astype(jnp.float32)
    )
    first_value, first_pull = jax.vjp(normalize, inputs, gain_one, shift_one)
    grad_inputs_norm, grad_gain_one, grad_shift_one = first_pull(grad_normed_one)
    input_gradient = grad_middle + grad_inputs_norm

    chunk = width // 2
    eight_grad = jnp.stack(
        [
            grad_gain_one, grad_shift_one, grad_query_bias, grad_value_bias,
            grad_out_bias, grad_gain_two, grad_shift_two, grad_down_bias,
        ]
    ).reshape(8, shards, rows).transpose(1, 0, 2).reshape(shards, 8 * rows)
    small_grad = jnp.concatenate([eight_grad, grad_up_bias.reshape(shards, -1)], axis=1)
    down_sum, up_sum, rest_sum, small_sum = reduce_call(
        fsdp,
        reps,
        (
            active[0], cotangent[0], normed_two[0], grad_hidden[0], normed_all[0],
            grad_query, grad_keys, grad_values, attended, grad_branch[0],
        ),
        small_grad[:, None],
    )

    def rows_of(summed):
        return summed.transpose(1, 0, 2).reshape(rows, -1)

    down_own = (
        down_sum.reshape(4, 2, rows, chunk).transpose(0, 2, 1, 3).reshape(4 * rows, width)
    )
    eight_own = small_sum[0, : 8 * rows].reshape(8, rows)
    return (
        layer_out,
        input_gradient,
        eight_own[0],
        eight_own[1],
        rows_of(rest_sum[:6]),
        eight_own[2],
        eight_own[3],
        rows_of(rest_sum[6:]),
        eight_own[4],
        eight_own[5],
        eight_own[6],
        rows_of(up_sum),
        small_sum[0, 8 * rows :],
        down_own,
        eight_own[7],
    )


def solution(mesh):
    placed = (
        P(("rep", "fsdp"), "seq", None),
        P(("rep", "fsdp"), "seq", None),
        P(("fsdp", "seq")),
        P(("fsdp", "seq")),
        P(("fsdp", "seq"), None),
        P(("fsdp", "seq")),
        P(("fsdp", "seq")),
        P(("fsdp", "seq"), None),
        P(("fsdp", "seq")),
        P(("fsdp", "seq")),
        P(("fsdp", "seq")),
        P(("fsdp", "seq"), None),
        P(("fsdp", "seq")),
        P(("fsdp", "seq"), None),
        P(("fsdp", "seq")),
    )
    return jax.shard_map(
        functools.partial(on_device, mesh.shape["fsdp"], mesh.shape["rep"]),
        mesh=mesh,
        in_specs=placed,
        out_specs=(
            P(("rep", "fsdp"), "seq", None),
            P(("rep", "fsdp"), "seq", None),
            P(("fsdp", "seq")),
            P(("fsdp", "seq")),
            P(("fsdp", "seq"), None),
            P(("fsdp", "seq")),
            P(("fsdp", "seq")),
            P(("fsdp", "seq"), None),
            P(("fsdp", "seq")),
            P(("fsdp", "seq")),
            P(("fsdp", "seq")),
            P(("fsdp", "seq"), None),
            P(("fsdp", "seq")),
            P(("fsdp", "seq"), None),
            P(("fsdp", "seq")),
        ),
        check_vma=False,
    )
```

```python
import functools
import math

import jax
import jax.numpy as jnp
from jax import lax
from jax.experimental import pallas as pl
from jax.experimental.pallas import tpu as pltpu
from jax.sharding import PartitionSpec as P

HEADS = 12


EPSILON = 1e-06


def normalize(features, scale_gain, shift_bias):
    row_mean = jnp.mean(features, axis=-1, keepdims=True)
    centred = features - row_mean
    row_var = jnp.mean(centred * centred, axis=-1, keepdims=True)
    return centred * lax.rsqrt(row_var + EPSILON) * scale_gain + shift_bias


def gelu_exact(features):
    return jax.nn.gelu(features, approximate=False)


def project(first_operand, second_operand):
    return jnp.einsum(
        "itk,kn->itn", first_operand, second_operand, preferred_element_type=jnp.float32
    )


def project_back(first_operand, second_operand):
    return jnp.einsum(
        "itn,kn->itk", first_operand, second_operand, preferred_element_type=jnp.float32
    )


MESH = pl.DeviceIdType.MESH
LIMIT = 60000 * 1024


def meet_all(axes_list):
    barrier = pltpu.get_barrier_semaphore()
    for place in axes_list:
        pl.semaphore_signal(barrier, inc=1, device_id=place, device_id_type=MESH)
    pl.semaphore_wait(barrier, len(axes_list))


def plane_peers(flat, shards):
    for step in range(1, shards):
        peer = lax.rem(flat + step, shards)
        yield step, {"fsdp": lax.div(peer, 2), "seq": lax.rem(peer, 2)}


class Sender:
    def __init__(self, send_sem, recv_sem):
        self.send_sem, self.recv_sem, self.used = send_sem, recv_sem, 0

    def __call__(self, source, target, place):
        index = self.used
        self.used += 1
        return pltpu.make_async_remote_copy(
            src_ref=source,
            dst_ref=target,
            send_sem=self.send_sem.at[index],
            recv_sem=self.recv_sem.at[index],
            device_id=place,
            device_id_type=MESH,
        )


def gather_body(fsdp, weights, outs, early, compute, send_sem, recv_sem, local_sem):
    count = len(weights)
    ys = fsdp // 2
    me_f, x = lax.axis_index("fsdp"), lax.axis_index("seq")
    y, c = lax.div(me_f, 2), lax.rem(me_f, 2)
    flat = me_f * 2 + x
    shards = fsdp * 2
    make = Sender(send_sem, recv_sem)

    def slot(yy, cc, xx):
        return (yy * 2 + cc) * 2 + xx

    at_x = {"fsdp": me_f, "seq": 1 - x}
    at_core = {"fsdp": y * 2 + 1 - c, "seq": x}
    at_y = [{"fsdp": lax.rem(y + j, ys) * 2 + c, "seq": x} for j in range(1, ys)]
    from_y = [lax.rem(y + ys - j, ys) for j in range(1, ys)]
    meet_all([place for _, place in plane_peers(flat, shards)])
    sent, awaited, local = [], [], []

    def go(copy):
        copy.start()
        sent.append(copy)
        return copy

    for index, (source, target) in enumerate(zip(weights, outs)):
        keep = pltpu.make_async_copy(source, target.at[flat], local_sem.at[index])
        keep.start()
        local.append(keep)
    if early is not None:
        small, small_out, images, images_out = early
        keep = pltpu.make_async_copy(small, small_out.at[flat], local_sem.at[count])
        keep.start()
        local.append(keep)
        for _, place in plane_peers(flat, shards):
            awaited.append(go(make(small, small_out.at[flat], place)))
        awaited.append(go(make(images, images_out, at_x)))
    first = []
    for source, target in zip(weights, outs):
        hand_x = go(make(source, target.at[flat], at_x))
        hand_y = [go(make(source, target.at[flat], place)) for place in at_y]
        awaited.append(go(make(source, target.at[flat], at_core)))
        first.append((hand_x, hand_y))
    second = []

    def relay_one(index):
        target = outs[index]
        half = weights[index].shape[1] // 2
        low, high = pl.ds(0, half), pl.ds(half, half)
        hand_x, hand_y = first[index]
        passed_y, passed_x = [], []
        hand_x.wait_recv()
        block = target.at[slot(y, c, 1 - x)]
        for place in at_y:
            part = block.at[:, low]
            passed_y.append(go(make(part, part, place)))
        awaited.append(go(make(block, block, at_core)))
        for yy, hand in zip(from_y, hand_y):
            hand.wait_recv()
            block = target.at[slot(yy, c, x)]
            part = block.at[:, high]
            passed_x.append(go(make(part, part, at_x)))
            awaited.append(go(make(block, block, at_core)))
        second.append((passed_y, passed_x))

    def relay_two(index):
        target = outs[index]
        half = weights[index].shape[1] // 2
        low, high = pl.ds(0, half), pl.ds(half, half)
        passed_y, passed_x = second[index]
        for yy, by_y, by_x in zip(from_y, passed_y, passed_x):
            block = target.at[slot(yy, c, 1 - x)]
            by_y.wait_recv()
            awaited.append(go(make(block.at[:, low], block.at[:, low], at_core)))
            by_x.wait_recv()
            awaited.append(go(make(block.at[:, high], block.at[:, high], at_core)))

    if compute is not None:
        compute()
    for index in range(count):
        relay_one(index)
        if index:
            relay_two(index - 1)
    relay_two(count - 1)
    for copy in awaited:
        copy.wait_recv()
    for copy in sent:
        copy.wait_send()
    for copy in local:
        copy.wait()


def gather_scratch(fsdp, count):
    copies = fsdp * 2 + count * (3 + 6 * (fsdp // 2 - 1) + 2)
    return [
        pltpu.SemaphoreType.DMA((copies,)),
        pltpu.SemaphoreType.DMA((copies,)),
        pltpu.SemaphoreType.DMA((count + 1,)),
    ]


def gather_first(fsdp, weight, pieces, images):
    shards = fsdp * 2
    extent = sum(p.shape[1] for p in pieces)
    number = len(pieces)

    def body(*refs):
        source, images_ref = refs[0], refs[1]
        vectors = refs[2 : 2 + number]
        target, small_out, images_out, small, *sems = refs[2 + number :]
        start = 0
        for vector in vectors:
            size = vector.shape[1]
            small[:, start : start + size] = vector[...].astype(jnp.float32)
            start += size
        early = (small, small_out, images_ref, images_out)
        gather_body(fsdp, [source], [target], early, None, *sems)

    return pl.pallas_call(
        body,
        out_shape=[
            jax.ShapeDtypeStruct((shards,) + weight.shape, weight.dtype),
            jax.ShapeDtypeStruct((shards, 1, extent), jnp.float32),
            jax.ShapeDtypeStruct(images.shape, images.dtype),
        ],
        in_specs=[pl.BlockSpec(memory_space=pltpu.VMEM)] * (number + 2),
        out_specs=[pl.BlockSpec(memory_space=pl.ANY)] * 3,
        scratch_shapes=[pltpu.VMEM((1, extent), jnp.float32)] + gather_scratch(fsdp, 1),
        compiler_params=pltpu.CompilerParams(
            collective_id=1, has_side_effects=True, vmem_limit_bytes=LIMIT
        ),
    )(weight, images, *pieces)


def gather_attend(fsdp, weights, normed_all, input_full, query_add, value_add):
    count = len(weights)
    shards = fsdp * 2
    keys_count, width = normed_all.shape
    tokens = keys_count // 2
    head = width // HEADS
    pairs = HEADS // 2
    scale = 1.0 / math.sqrt(head)
    low = jnp.bfloat16

    def body(*refs):
        sources = refs[:count]
        normed, whole_in, query_bias, value_bias = refs[count : count + 4]
        targets = refs[count + 4 : 2 * count + 4]
        query, keys, values, out, logsum = refs[2 * count + 4 : 2 * count + 9]
        sems = refs[2 * count + 9 :]

        def mix(step, carry):
            at = pl.multiple_of(step * 256, 128)
            here = pl.ds(at, 256)
            rows = normed[...]
            query[:, here] = (
                jnp.dot(rows[:tokens], whole_in[:, here], preferred_element_type=jnp.float32)
                + query_bias[:, here]
            ).astype(low)
            keys[:, here] = jnp.dot(
                rows,
                whole_in[:, pl.ds(pl.multiple_of(at + width, 128), 256)],
                preferred_element_type=jnp.float32,
            ).astype(low)
            values[:, here] = (
                jnp.dot(
                    rows,
                    whole_in[:, pl.ds(pl.multiple_of(at + 2 * width, 128), 256)],
                    preferred_element_type=jnp.float32,
                )
                + value_bias[:, here]
            ).astype(low)
            return carry

        def attend(pair, carry):
            here = pl.ds(pl.multiple_of(pair * 2 * head, 128), 2 * head)
            q2, k2, v2 = query[:, here], keys[:, here], values[:, here]
            results = []
            for part in range(2):
                at = slice(part * head, (part + 1) * head)
                scores = scale * lax.dot_general(
                    q2[:, at], k2[:, at], (((1,), (1,)), ((), ())),
                    preferred_element_type=jnp.float32,
                )
                peak = jnp.max(scores, axis=-1, keepdims=True)
                shifted = jnp.exp(scores - peak)
                total = jnp.sum(shifted, axis=-1, keepdims=True)
                probs = (shifted * (1.0 / total)).astype(low)
                results.append(
                    jnp.dot(probs, v2[:, at], preferred_element_type=jnp.float32)
                )
                logsum[pair, :, part : part + 1] = peak + jnp.log(total)
            out[:, here] = jnp.concatenate(results, axis=1).astype(low)
            return carry

        def compute():
            lax.fori_loop(0, width // 256, mix, 0)
            lax.fori_loop(0, pairs, attend, 0)

        gather_body(fsdp, sources, targets, None, compute, *sems)

    inside = pl.BlockSpec(memory_space=pltpu.VMEM)
    return pl.pallas_call(
        body,
        out_shape=[jax.ShapeDtypeStruct((shards,) + w.shape, w.dtype) for w in weights]
        + [
            jax.ShapeDtypeStruct((tokens, width), low),
            jax.ShapeDtypeStruct((keys_count, width), low),
            jax.ShapeDtypeStruct((keys_count, width), low),
            jax.ShapeDtypeStruct((tokens, width), low),
            jax.ShapeDtypeStruct((pairs, tokens, 2), jnp.float32),
        ],
        in_specs=[inside] * (count + 4),
        out_specs=[pl.BlockSpec(memory_space=pl.ANY)] * count + [inside] * 5,
        scratch_shapes=gather_scratch(fsdp, count),
        compiler_params=pltpu.CompilerParams(
            collective_id=3, has_side_effects=True, vmem_limit_bytes=LIMIT
        ),
    )(*weights, normed_all, input_full, query_add, value_add)


def reduce_body(fsdp, reps, groups, *refs):
    low = jnp.bfloat16
    (
        active, cot, normed_two, grad_hidden, normed_all,
        grad_query, grad_keys, grad_values, attended, grad_branch, small,
    ) = refs[:11]
    outs, small_out = refs[11 : 11 + groups], refs[11 + groups]
    at = 12 + groups
    got_core, got_a1, got_b1, got_a2, got_b2, whole, got_z, kept_z, parts = [
        refs[at + i * groups : at + (i + 1) * groups] for i in range(9)
    ]
    small_got, small_sum, small_z, send_sem, recv_sem = refs[at + 9 * groups :]
    ys = fsdp // 2
    shards = fsdp * 2
    units = 8
    share = units // reps
    me_f, x, z = lax.axis_index("fsdp"), lax.axis_index("seq"), lax.axis_index("rep")
    y, c = lax.div(me_f, 2), lax.rem(me_f, 2)
    flat = me_f * 2 + x
    at_x = {"fsdp": me_f, "seq": 1 - x}
    at_core = {"fsdp": y * 2 + 1 - c, "seq": x}
    to_y = [lax.rem(y + j, ys) for j in range(1, ys)]
    at_y = [{"fsdp": yy * 2 + c, "seq": x} for yy in to_y]
    to_z = [lax.rem(z + d, reps) for d in range(1, reps)]
    at_z = [{"rep": zz} for zz in to_z]
    make = Sender(send_sem, recv_sem)
    sent = []

    def go(copy):
        copy.start()
        sent.append(copy)
        return copy

    meet_all([place for _, place in plane_peers(flat, shards)] + at_z)

    def loop(extent, step):
        lax.fori_loop(0, extent, lambda i, carry: (step(i), carry)[1], 0)

    core_hand = {}
    tokens = cot.shape[0]
    rows, chunk = parts[0].shape[-2:]

    def outer(left, right):
        return lax.dot_general(
            left, right, (((0,), (0,)), ((), ())), preferred_element_type=jnp.float32
        )

    def columns(part, first, left, right):
        def one(u):
            start = pl.multiple_of(u * chunk, 128)
            total = outer(left[...], right[:, pl.ds(start, chunk)])
            part[first + u] = total.reshape(ys, 2, 2, rows, chunk).astype(low)

        loop(right.shape[1] // chunk, one)

    def stage_grads(g):
        part = parts[g]
        if g == 0:
            width = cot.shape[1]
            per = width // (4 * rows)

            def one(block):
                start = pl.multiple_of(block * width, 128)
                total = outer(active[:, pl.ds(start, width)], cot[...])
                for near in range(per):
                    owner = block * per + near
                    yy, cc, xx = lax.div(owner, 4), lax.rem(lax.div(owner, 2), 2), lax.rem(owner, 2)
                    for i in range(4):
                        top = (near * 4 + i) * rows
                        for j in range(2):
                            part[i * 2 + j, yy, cc, xx] = total[
                                top : top + rows, j * chunk : (j + 1) * chunk
                            ].astype(low)

            loop(active.shape[1] // width, one)
        elif g == 1:
            columns(part, 0, normed_two, grad_hidden)
        else:
            columns(part, 0, normed_all.at[pl.ds(0, tokens)], grad_query)
            columns(part, 2, normed_all, grad_keys)
            columns(part, 4, normed_all, grad_values)
            columns(part, 6, attended, grad_branch)
        core_hand[g] = go(make(part.at[:, :, 1 - c], got_core[g], at_core))

    small_hand = []
    for step, place in plane_peers(flat, shards):
        peer = lax.rem(flat + step, shards)
        small_hand.append(go(make(small.at[peer], small_got.at[step - 1], place)))
    hands = {}

    def stage_core(g):
        core_hand[g].wait_recv()
        got, part = got_core[g], parts[g]

        def add(i):
            u, rest = lax.div(i, 2 * ys), lax.rem(i, 2 * ys)
            yy, xx = lax.div(rest, 2), lax.rem(rest, 2)
            got[u, yy, xx] = got[u, yy, xx] + part[u, yy, c, xx]

        loop(units * 2 * ys, add)
        a1 = go(make(got.at[pl.ds(0, 4), :, 1 - x], got_a1[g], at_x))
        b1 = [
            go(make(got.at[pl.ds(4, 4), yy], got_b1[g].at[j], place))
            for j, (yy, place) in enumerate(zip(to_y, at_y))
        ]
        hands[g] = [a1, b1]

    def stage_cross(g):
        a1, b1 = hands[g]
        got, from_x, from_y = got_core[g], got_a1[g], got_b1[g]
        a1.wait_recv()

        def add_a(i):
            u, yy = lax.div(i, ys), lax.rem(i, ys)
            got[u, yy, x] = got[u, yy, x] + from_x[u, yy]

        loop(4 * ys, add_a)
        a2 = [
            go(make(got.at[pl.ds(0, 4), yy, x], got_a2[g].at[j], place))
            for j, (yy, place) in enumerate(zip(to_y, at_y))
        ]
        for copy in b1:
            copy.wait_recv()

        def add_b(i):
            u, xx = lax.div(i, 2), lax.rem(i, 2)
            total = got[u + 4, y, xx].astype(jnp.float32)
            for j in range(ys - 1):
                total = total + from_y[j, u, xx].astype(jnp.float32)
            got[u + 4, y, xx] = total.astype(low)

        loop(8, add_b)
        b2 = go(make(got.at[pl.ds(4, 4), y, 1 - x], got_b2[g], at_x))
        hands[g] = [a2, b2]

    def stage_own(g):
        a2, b2 = hands[g]
        got, from_y, from_x, total_ref = got_core[g], got_a2[g], got_b2[g], whole[g]
        for copy in a2:
            copy.wait_recv()

        def add_a(u):
            total = got[u, y, x].astype(jnp.float32)
            for j in range(ys - 1):
                total = total + from_y[j, u].astype(jnp.float32)
            total_ref[u] = total.astype(low)

        loop(4, add_a)
        b2.wait_recv()

        def add_b(u):
            total_ref[u + 4] = got[u + 4, y, x] + from_x[u]

        loop(4, add_b)
        hands[g] = [
            go(make(total_ref.at[pl.ds(zz * share, share)], got_z[g].at[d], place))
            for d, (zz, place) in enumerate(zip(to_z, at_z))
        ]

    def stage_rep(g):
        for copy in hands[g]:
            copy.wait_recv()
        total_ref, from_z, kept = whole[g], got_z[g], kept_z[g]

        def add(u):
            total = total_ref[z * share + u].astype(jnp.float32)
            for d in range(reps - 1):
                total = total + from_z[d, u].astype(jnp.float32)
            kept[z * share + u] = total.astype(low)

        loop(share, add)
        mine = kept.at[pl.ds(z * share, share)]
        hands[g] = [go(make(mine, mine, place)) for place in at_z]

    def stage_end(g):
        for copy in hands[g]:
            copy.wait_recv()
        kept, out = kept_z[g], outs[g]

        def widen(u):
            out[u] = kept[u].astype(jnp.float32)

        loop(units, widen)

    stages = (stage_grads, stage_core, stage_cross, stage_own, stage_rep, stage_end)
    for tick in range(groups + len(stages) - 1):
        if tick == groups:
            for copy in small_hand:
                copy.wait_recv()
            total = small[flat]
            for step in range(shards - 1):
                total = total + small_got[step]
            small_sum[...] = total
            small_hand_z = [
                go(make(small_sum, small_z.at[d], place)) for d, place in enumerate(at_z)
            ]
        for number, stage in enumerate(stages):
            g = tick - number
            if 0 <= g < groups:
                stage(g)
    for copy in small_hand_z:
        copy.wait_recv()
    total = small_sum[...]
    for d in range(reps - 1):
        total = total + small_z[d]
    small_out[...] = total
    for copy in sent:
        copy.wait_send()


def reduce_call(fsdp, reps, operands, small):
    groups = 3
    shards, ys = fsdp * 2, fsdp // 2
    units, rows, width = 8, operands[1].shape[1] // shards, operands[1].shape[1] // 2
    share = units // reps
    copies = (shards - 1) + (reps - 1) + groups * (1 + 1 + (ys - 1) * 2 + 1 + 2 * (reps - 1))
    low = jnp.bfloat16

    def many(*lead):
        return [pltpu.VMEM(lead + (rows, width), low)] * groups

    scratch = (
        many(units, ys, 2)
        + many(4, ys)
        + many(ys - 1, 4, 2)
        + many(ys - 1, 4)
        + many(4)
        + many(units)
        + many(reps - 1, share)
        + many(units)
        + many(units, ys, 2, 2)
        + [
            pltpu.VMEM((shards - 1,) + small.shape[1:], jnp.float32),
            pltpu.VMEM(small.shape[1:], jnp.float32),
            pltpu.VMEM((reps - 1,) + small.shape[1:], jnp.float32),
            pltpu.SemaphoreType.DMA((copies,)),
            pltpu.SemaphoreType.DMA((copies,)),
        ]
    )
    return pl.pallas_call(
        lambda *refs: reduce_body(fsdp, reps, groups, *refs),
        out_shape=[jax.ShapeDtypeStruct((units, rows, width), jnp.float32)] * groups
        + [jax.ShapeDtypeStruct(small.shape[1:], jnp.float32)],
        in_specs=[pl.BlockSpec(memory_space=pltpu.VMEM)] * 11,
        out_specs=[pl.BlockSpec(memory_space=pltpu.VMEM)] * (groups + 1),
        scratch_shapes=scratch,
        compiler_params=pltpu.CompilerParams(
            collective_id=2, has_side_effects=True, vmem_limit_bytes=LIMIT
        ),
    )(*operands, small)


def attend_back_body(
    scale, head, query, keys, values, grad, logsum, grad_query, grad_keys, grad_values
):
    low = jnp.bfloat16

    def dot(left, right, left_dim, right_dim):
        return lax.dot_general(
            left, right, (((left_dim,), (right_dim,)), ((), ())),
            preferred_element_type=jnp.float32,
        )

    for part in range(2):
        at = slice(part * head, (part + 1) * head)
        q, k, v, g = query[:, at], keys[:, at], values[:, at], grad[:, at]
        weights = jnp.exp(scale * dot(q, k, 1, 1) - logsum[0, :, part : part + 1])
        grad_weights = dot(g, v, 1, 1)
        inner = jnp.sum(weights * grad_weights, axis=-1, keepdims=True)
        grad_scores = (weights * (grad_weights - inner)).astype(low)
        grad_query[:, at] = (scale * dot(grad_scores, k, 1, 0)).astype(low)
        grad_keys[:, at] = (scale * dot(grad_scores, q, 0, 0)).astype(low)
        grad_values[:, at] = dot(weights.astype(low), g, 0, 0).astype(low)


def attend_back_call(query, keys, values, grad, logsum):
    tokens, width = query.shape
    head = width // HEADS
    pairs = HEADS // 2
    mine = pl.BlockSpec((tokens, 2 * head), lambda i: (0, i))
    full = pl.BlockSpec((keys.shape[0], 2 * head), lambda i: (0, i))
    return pl.pallas_call(
        functools.partial(attend_back_body, 1.0 / math.sqrt(head), head),
        grid=(pairs,),
        out_shape=[
            jax.ShapeDtypeStruct(query.shape, jnp.bfloat16),
            jax.ShapeDtypeStruct(keys.shape, jnp.bfloat16),
            jax.ShapeDtypeStruct(keys.shape, jnp.bfloat16),
        ],
        in_specs=[mine, full, full, mine, pl.BlockSpec((1, tokens, 2), lambda i: (i, 0, 0))],
        out_specs=[mine, full, full],
    )(query, keys, values, grad, logsum)


def on_device(
    fsdp,
    reps,
    images,
    cotangent,
    first_gain,
    first_shift,
    input_weight,
    query_bias,
    value_bias,
    output_weight,
    output_bias,
    second_gain,
    second_shift,
    up_weight,
    up_bias,
    down_weight,
    down_bias,
):
    feature_width = images.shape[2]
    pieces = (
        first_gain, first_shift, query_bias, value_bias, output_bias,
        second_gain, second_shift, down_bias, up_bias,
    )
    shards = fsdp * 2
    input_full, small_full, images_other = gather_first(
        fsdp, input_weight, [p[None] for p in pieces], images[0]
    )
    input_full = input_full.reshape(-1, input_full.shape[-1])
    rows = first_gain.shape[0]
    small_full = small_full.reshape(shards, -1)
    eight = small_full[:, : 8 * rows].reshape(shards, 8, rows).transpose(1, 0, 2).reshape(8, -1)
    gain_one, shift_one, query_add, value_add, output_add, gain_two, shift_two, down_add = [
        eight[i] for i in range(8)
    ]
    up_add = small_full[:, 8 * rows :].reshape(-1)

    inputs = images.astype(jnp.float32)
    normed_one = normalize(inputs, gain_one, shift_one).astype(jnp.bfloat16)
    normed_other = normalize(
        images_other[None].astype(jnp.float32), gain_one, shift_one
    ).astype(jnp.bfloat16)
    normed_all = jnp.concatenate([normed_one, normed_other], axis=1)
    width = feature_width
    tokens = images.shape[1]
    *fulls, query_local, keys_all, values_all, attended, logsum = gather_attend(
        fsdp,
        (output_weight, up_weight, down_weight),
        normed_all[0],
        input_full,
        query_add[None],
        value_add[None],
    )
    output_full, up_full, down_full = [w.reshape(-1, w.shape[-1]) for w in fulls]
    attended_local = attended[None]
    middle = inputs + project(attended_local, output_full) + output_add
    normed_two = normalize(middle, gain_two, shift_two).astype(jnp.bfloat16)
    hidden = project(normed_two, up_full) + up_add
    active = gelu_exact(hidden).astype(jnp.bfloat16)
    branch_sum = project(active, down_full)
    layer_out = (middle + branch_sum + down_add).astype(jnp.bfloat16)

    grad_down_bias = jnp.sum(cotangent, axis=(0, 1), dtype=jnp.float32)
    grad_active = project_back(cotangent, down_full)
    gelu_value, gelu_pull = jax.vjp(gelu_exact, hidden)
    grad_hidden = gelu_pull(grad_active)[0].astype(jnp.bfloat16)
    grad_up_bias = jnp.sum(grad_hidden, axis=(0, 1), dtype=jnp.float32)
    grad_normed_two = project_back(grad_hidden, up_full)
    norm_value, second_pull = jax.vjp(normalize, middle, gain_two, shift_two)
    grad_middle_norm, grad_gain_two, grad_shift_two = second_pull(grad_normed_two)
    grad_middle = cotangent.astype(jnp.float32) + grad_middle_norm
    grad_branch = grad_middle.astype(jnp.bfloat16)
    grad_out_bias = jnp.sum(grad_branch, axis=(0, 1), dtype=jnp.float32)
    grad_attended = project_back(grad_branch, output_full).astype(jnp.bfloat16)
    grad_query, grad_keys, grad_values = attend_back_call(
        query_local, keys_all, values_all, grad_attended[0], logsum
    )
    grad_query_bias = jnp.sum(grad_query, axis=0, dtype=jnp.float32)
    grad_value_bias = jnp.sum(grad_values, axis=0, dtype=jnp.float32)
    grad_normed_kv = project_back(grad_keys[None], input_full[:, width : 2 * width])
    grad_normed_kv = grad_normed_kv + project_back(grad_values[None], input_full[:, 2 * width :])
    to_other = grad_normed_kv[:, tokens:].astype(jnp.bfloat16)
    from_other = lax.ppermute(to_other, "seq", [(0, 1), (1, 0)])
    grad_normed_one = (
        grad_normed_kv[:, :tokens]
        + project_back(grad_query[None], input_full[:, :width])
        + from_other.astype(jnp.float32)
    )
    first_value, first_pull = jax.vjp(normalize, inputs, gain_one, shift_one)
    grad_inputs_norm, grad_gain_one, grad_shift_one = first_pull(grad_normed_one)
    input_gradient = grad_middle + grad_inputs_norm

    chunk = width // 2
    eight_grad = jnp.stack(
        [
            grad_gain_one, grad_shift_one, grad_query_bias, grad_value_bias,
            grad_out_bias, grad_gain_two, grad_shift_two, grad_down_bias,
        ]
    ).reshape(8, shards, rows).transpose(1, 0, 2).reshape(shards, 8 * rows)
    small_grad = jnp.concatenate([eight_grad, grad_up_bias.reshape(shards, -1)], axis=1)
    down_sum, up_sum, rest_sum, small_sum = reduce_call(
        fsdp,
        reps,
        (
            active[0], cotangent[0], normed_two[0], grad_hidden[0], normed_all[0],
            grad_query, grad_keys, grad_values, attended, grad_branch[0],
        ),
        small_grad[:, None],
    )

    def rows_of(summed):
        return summed.transpose(1, 0, 2).reshape(rows, -1)

    down_own = (
        down_sum.reshape(4, 2, rows, chunk).transpose(0, 2, 1, 3).reshape(4 * rows, width)
    )
    eight_own = small_sum[0, : 8 * rows].reshape(8, rows)
    return (
        layer_out,
        input_gradient,
        eight_own[0],
        eight_own[1],
        rows_of(rest_sum[:6]),
        eight_own[2],
        eight_own[3],
        rows_of(rest_sum[6:]),
        eight_own[4],
        eight_own[5],
        eight_own[6],
        rows_of(up_sum),
        small_sum[0, 8 * rows :],
        down_own,
        eight_own[7],
    )


def solution(mesh):
    placed = (
        P(("rep", "fsdp"), "seq", None),
        P(("rep", "fsdp"), "seq", None),
        P(("fsdp", "seq")),
        P(("fsdp", "seq")),
        P(("fsdp", "seq"), None),
        P(("fsdp", "seq")),
        P(("fsdp", "seq")),
        P(("fsdp", "seq"), None),
        P(("fsdp", "seq")),
        P(("fsdp", "seq")),
        P(("fsdp", "seq")),
        P(("fsdp", "seq"), None),
        P(("fsdp", "seq")),
        P(("fsdp", "seq"), None),
        P(("fsdp", "seq")),
    )
    return jax.shard_map(
        functools.partial(on_device, mesh.shape["fsdp"], mesh.shape["rep"]),
        mesh=mesh,
        in_specs=placed,
        out_specs=(
            P(("rep", "fsdp"), "seq", None),
            P(("rep", "fsdp"), "seq", None),
            P(("fsdp", "seq")),
            P(("fsdp", "seq")),
            P(("fsdp", "seq"), None),
            P(("fsdp", "seq")),
            P(("fsdp", "seq")),
            P(("fsdp", "seq"), None),
            P(("fsdp", "seq")),
            P(("fsdp", "seq")),
            P(("fsdp", "seq")),
            P(("fsdp", "seq"), None),
            P(("fsdp", "seq")),
            P(("fsdp", "seq"), None),
            P(("fsdp", "seq")),
        ),
        check_vma=False,
    )
```
